768 devices in a mesh: seq: 128 (over x, z_hi, y, core), wt: 6 (over z_lo).
Axes of the slice: x: 4, y: 8, z: 12 (z_hi: 2, z_lo: 6; z = z_hi * 6 + z_lo), core: 2. Of those that a mesh axis runs over, the one named last changes fastest.
Arguments:
- hidden_rows: bfloat16 [32768, 2688], P('seq'), may hold values from -24 to 24
- value_weight: bfloat16 [2688, 1536], P('seq', 'wt'), may hold values from -0.125 to 0.125
- queries: bfloat16 [32768, 3072], P('seq', 'wt'), may hold values from -60 to 60
- key_rows: bfloat16 [32768, 1536], P('seq', 'wt'), may hold values from -4.1 to 4.1
- out_grad: bfloat16 [32768, 3072], P('seq', 'wt'), may hold values from -6 to 6
- segments: int32 [32768], replicated, may hold values from 0 to 15, never falling along the last dimension, each value on 1 to 4096 neighbouring positions
Outputs:
- attention: bfloat16 [32768, 3072], P('seq', 'wt')
- weight_grad: float32 [2688, 1536], P('seq', 'wt')
The draws below stay inside these ranges and needn't reach their ends.
Inputs may be any that keep to these rules, and one draw needn't show every extreme that they name: `segments`: never falling along the slab.
All inputs are finite; a program needn't handle non-finite values.
Results may differ from the reference program's by a relative error of at most 0.0057.
Values may be sent and summed in bfloat16 or wider, within the bound.
No kernel may reach another device: no remote copies, remote signals or barrier semaphores. Data moves between devices by JAX's collectives and lax.ppermute only.
A program may use at most 32 MiB of HBM per device.

```python
import math
import jax
import jax.numpy as jnp
import numpy as np
from jax import lax

D = 2688
H = 24
KVH = 12
HD = 128
WINDOW = 1024
TOK_DEV = 256
TOKENS = 32768
REACH = 4


def shared_draw(key):
    base = jax.random.fold_in(key, 4242)
    key_first, key_second = jax.random.split(base, 2)
    key_part = jnp.clip(jax.random.normal(key_first, (TOKENS, KVH * HD), jnp.float32), -4.0, 4.0)
    query_part = jnp.clip(jax.random.normal(key_second, (TOKENS, H * HD), jnp.float32), -4.0, 4.0)
    return (query_part, key_part)


def draw_queries(key, part):
    return shared_draw(key)[0].astype(jnp.bfloat16)


def draw_key_rows(key, part):
    return shared_draw(key)[1].astype(jnp.bfloat16)


def raised(values, own_key, source, target, parts, factor):
    owner, partner = [(jnp.arange(values.shape[position]) // (values.shape[position] // parts)).reshape([-1 if axis == position else 1 for axis in range(values.ndim)]) for position in (source, target)]
    chosen = jax.random.permutation(own_key, parts)[partner]
    strong = (owner == chosen) | (owner == (partner + parts // 2) % parts)
    return jnp.where(strong, factor * values, values)


def shard_levels(own_key, extent, pieces, least, top_value):
    def one(position, parts):
        draws = jax.random.uniform(jax.random.fold_in(jax.random.fold_in(own_key, 6), position), (parts,), jnp.float32, least / len(pieces), top_value / len(pieces))
        return jnp.repeat(jnp.exp(draws), extent[position] // parts).reshape((-1,) + (1,) * (len(extent) - position - 1))

    loudness = one(*pieces[0])
    for cut in pieces[1:]:
        loudness = loudness * one(*cut)
    return loudness


def split_up(number_of, total, bound, slope):
    portions = [(1 << 20) // math.isqrt(rank ** slope) + 1 for rank in range(2, number_of + 1)]
    surplus, counts = total - bound - (number_of - 1), [1] * (number_of - 1)
    while surplus > 0:
        movable = [i for i in range(number_of - 1) if counts[i] < bound]
        whole, left = sum([portions[i] for i in movable]), surplus
        for i in movable:
            addition = min(bound - counts[i], max(1, left * portions[i] // whole), surplus)
            counts[i] = counts[i] + addition
            surplus = surplus - addition
    return np.array([bound] + counts)


def uneven(stream_key, number_of, total, bound, skew):
    if number_of == 2:
        one = jax.random.randint(stream_key, (), max(1, total - bound), min(bound, total - 1) + 1)
        return jnp.stack([one, total - one])
    lengths = jnp.asarray(split_up(number_of, total, bound, skew), jnp.int32)
    couples = (number_of - 1) // 2
    donor, taker = lengths[1:1 + 2 * couples:2], lengths[2:2 + 2 * couples:2]
    room = jnp.minimum(donor - 1, bound - taker)
    moved = jax.random.randint(jax.random.fold_in(stream_key, 1), (couples,), 0, 1 << 20) % (room + 1)
    lengths = lengths.at[1:1 + 2 * couples:2].set(donor - moved).at[2:2 + 2 * couples:2].set(taker + moved)
    return lengths[jax.random.permutation(jax.random.fold_in(stream_key, 2), number_of)]


def centred(stream_key, dims, deviation, limit, cuts=(), kind=jnp.bfloat16):
    array = deviation * jax.random.normal(stream_key, dims, jnp.float32)
    if cuts:
        array = array * shard_levels(stream_key, dims, cuts, -0.22, 0.18)
    return jnp.clip(array, -limit, limit).astype(kind)


def heavy_noise(key, shape, width, bound, cuts, heavy, kind=jnp.bfloat16):
    drawn = width * jax.random.normal(key, shape, jnp.float32)
    if cuts:
        drawn = drawn * shard_levels(key, shape, cuts, -0.22, 0.18)
    return jnp.clip(raised(drawn, jax.random.fold_in(key, 3), *heavy), -bound, bound).astype(kind)


def setup_inputs(seed: int = 0) -> dict:
    key_list = jax.random.split(jax.random.key(seed), 7)
    return {
        "hidden_rows": heavy_noise(key_list[0], (TOKENS, D), 1.0, 24.0, ((0, 128),), (0, 1, 128, 5.5)),
        "value_weight": centred(key_list[1], (D, KVH * HD), D ** -0.5, 0.125, ((0, 128), (1, 6))),
        "queries": draw_queries(jax.random.fold_in(key_list[6], 71), 0),
        "key_rows": draw_key_rows(jax.random.fold_in(key_list[6], 71), 0),
        "out_grad": centred(key_list[4], (TOKENS, H * HD), 1.0, 6.0, ((0, 128), (1, 6))),
        "segments": jnp.searchsorted(jnp.cumsum(uneven(key_list[5], max(2, TOKENS // (2 * WINDOW)), TOKENS, min(4 * WINDOW, TOKENS // 2), 0)), jnp.arange(TOKENS), side="right").astype(jnp.int32),
    }


def reference(hidden_rows, value_weight, queries, key_rows, out_grad, segments):
    rows_here = TOK_DEV
    blocks_back = REACH
    key_span = (blocks_back + 1) * rows_here
    padding = blocks_back * rows_here
    group_size = H // KVH
    kv_width = KVH * HD
    scale = 1.0 / math.sqrt(HD)
    values = jnp.dot(hidden_rows, value_weight, preferred_element_type=jnp.float32).astype(jnp.bfloat16)
    keys_padded = jnp.concatenate([jnp.zeros((padding, kv_width), jnp.bfloat16), key_rows], axis=0)
    values_padded = jnp.concatenate([jnp.zeros((padding, kv_width), jnp.bfloat16), values], axis=0)
    segs_padded = jnp.concatenate([jnp.full((padding,), -1, jnp.int32), segments.astype(jnp.int32)], axis=0)
    distance = jnp.arange(rows_here, dtype=jnp.int32)[:, None] + padding - jnp.arange(key_span, dtype=jnp.int32)[None, :]

    def one_block(carried, block_index):
        anchor = (block_index * rows_here).astype(jnp.int32)
        query_four = lax.dynamic_slice_in_dim(queries, anchor, rows_here, 0).reshape(rows_here, KVH, group_size, HD).astype(jnp.float32)
        grad_four = lax.dynamic_slice_in_dim(out_grad, anchor, rows_here, 0).reshape(rows_here, KVH, group_size, HD).astype(jnp.float32)
        key_three = lax.dynamic_slice_in_dim(keys_padded, anchor, key_span, 0).reshape(key_span, KVH, HD).astype(jnp.float32)
        value_three = lax.dynamic_slice_in_dim(values_padded, anchor, key_span, 0).reshape(key_span, KVH, HD).astype(jnp.float32)
        query_seg = lax.dynamic_slice_in_dim(segments.astype(jnp.int32), anchor, rows_here, 0)
        key_seg = lax.dynamic_slice_in_dim(segs_padded, anchor, key_span, 0)
        allowed = (distance >= 0) & (distance < WINDOW) & (query_seg[:, None] == key_seg[None, :])
        scores = jnp.einsum('tkgd,lkd->kgtl', query_four, key_three) * scale
        scores = jnp.where(allowed[None, None], scores, -1e+30)
        highest = lax.optimization_barrier(jnp.max(scores, axis=-1, keepdims=True))
        weights = jnp.exp(scores - highest)
        probs = (weights / lax.optimization_barrier(jnp.sum(weights, axis=-1, keepdims=True))).astype(jnp.bfloat16)
        probs_wide = probs.astype(jnp.float32)
        output = jnp.einsum('kgtl,lkd->tkgd', probs_wide, value_three).reshape(rows_here, H * HD).astype(jnp.bfloat16)
        partial_value = jnp.einsum('kgtl,tkgd->lkd', probs_wide, grad_four).reshape(key_span, kv_width).astype(jnp.bfloat16)
        current = lax.dynamic_slice_in_dim(carried, anchor, key_span, 0)
        carried = lax.dynamic_update_slice_in_dim(carried, current + partial_value.astype(jnp.float32), anchor, 0)
        return (carried, output)
    initial = jnp.zeros((padding + TOKENS, kv_width), jnp.float32)
    summed, outputs = lax.scan(one_block, initial, jnp.arange(TOKENS // rows_here, dtype=jnp.int32))
    attention = outputs.reshape(TOKENS, H * HD)
    value_grad = summed[padding:].astype(jnp.bfloat16)
    weight_grad = jnp.dot(hidden_rows.T, value_grad, preferred_element_type=jnp.float32)
    return (attention, weight_grad)
```

```python
import math

import jax
import jax.numpy as jnp
from jax import lax
from jax.sharding import Mesh, PartitionSpec as P

HD = 128
WINDOW = 1024
GRID = ("x", "zh", "y", "c")
CHIPS = ("x", "zh", "y")
SWAP = [(0, 1), (1, 0)]
SIZES = (4, 2, 8, 2)


def chip_shift(block, distance):
    chips = lax.axis_size("x") * lax.axis_size("zh") * lax.axis_size("y")
    route = [(i - distance, i) for i in range(chips) if 0 <= i - distance < chips]
    return lax.ppermute(block, CHIPS, route)


def ordered(first, own, other, axis=0):
    return jnp.concatenate(
        [jnp.where(first, own, other), jnp.where(first, other, own)], axis=axis
    )


def per_device(hidden, weight, queries, keys, grads, segments):
    rows = hidden.shape[0]
    chip_rows = 2 * rows
    kv = weight.shape[1] // 2
    qw = queries.shape[1] // 2
    group = qw // kv
    nx, nz, ny = (lax.axis_size(a) for a in CHIPS)
    first = lax.axis_index("c") == 0
    low = lax.axis_index("zh") == 0
    chip = (lax.axis_index("x") * nz + lax.axis_index("zh")) * ny + lax.axis_index("y")
    scale = 1.0 / math.sqrt(HD)

    def halves(a):
        w = a.shape[1] // 2
        return jnp.where(first, a[:, :w], a[:, w:]), jnp.where(first, a[:, w:], a[:, :w])

    k_own, k_send = halves(keys)
    q_own, q_send = halves(queries)
    g_own, g_send = halves(grads)
    w_own, w_send = halves(weight)

    own = jnp.concatenate([k_own, q_own, g_own], axis=1)
    got = lax.ppermute(jnp.concatenate([k_send, q_send, g_send], axis=1), "c", SWAP)
    both = ordered(first, own, got)
    k_chip, q_chip, g_chip = both[:, :kv], both[:, kv : kv + qw], both[:, kv + qw :]
    k_win = jnp.concatenate([chip_shift(k_chip, 2), chip_shift(k_chip, 1), k_chip], axis=0)

    w_chip = ordered(first, w_own, lax.ppermute(w_send, "c", SWAP))
    w_pair = ordered(low, w_chip[None], lax.ppermute(w_chip, "zh", SWAP)[None])
    w_y = lax.all_to_all(jnp.broadcast_to(w_pair[None], (ny, *w_pair.shape)), "y", 0, 0)
    w_all = lax.all_to_all(jnp.broadcast_to(w_y[None], (nx, *w_y.shape)), "x", 0, 0)
    w_full = w_all.transpose(0, 2, 1, 3, 4).reshape(-1, kv)

    hidden_got = lax.ppermute(hidden, "c", SWAP)

    span = WINDOW + rows
    start = chip * chip_rows
    padding = 2 * chip_rows
    padded = jnp.concatenate([jnp.full((padding,), -1, jnp.int32), segments], axis=0)
    seg_win = lax.dynamic_slice_in_dim(padded, start, padding + chip_rows, 0)
    q_seg = seg_win[padding:].reshape(2, rows)
    k_seg = jnp.stack([seg_win[:span], seg_win[rows : rows + span]])
    distance = (
        jnp.arange(rows, dtype=jnp.int32)[:, None]
        + WINDOW
        - jnp.arange(span, dtype=jnp.int32)[None, :]
    )
    near = (distance >= 0) & (distance < WINDOW)
    allowed = near[None] & (q_seg[:, :, None] == k_seg[:, None, :])
    k_two = jnp.stack([k_win[:span], k_win[rows : rows + span]])
    q_four = q_chip.reshape(2, rows, group, HD)
    g_four = g_chip.reshape(2, rows, group, HD)
    scores = jnp.einsum("btgd,bld->bgtl", q_four, k_two, preferred_element_type=jnp.float32) * scale
    scores = jnp.where(allowed[:, None], scores, -1e30)
    highest = jnp.max(scores, axis=-1, keepdims=True)
    weights = jnp.exp(scores - highest)
    probs = (weights / jnp.sum(weights, axis=-1, keepdims=True)).astype(jnp.bfloat16)
    part = jnp.einsum("bgtl,btgd->bld", probs, g_four, preferred_element_type=jnp.float32)
    part = jnp.pad(part[0], ((0, rows), (0, 0))) + jnp.pad(part[1], ((rows, 0), (0, 0)))

    back2 = chip_shift(part[:chip_rows].astype(jnp.bfloat16), -2)
    back1 = chip_shift(part[chip_rows : 2 * chip_rows].astype(jnp.bfloat16), -1)
    value_grad = (
        part[2 * chip_rows :] + back1.astype(jnp.float32) + back2.astype(jnp.float32)
    ).astype(jnp.bfloat16)
    vg_own = jnp.where(first, value_grad[:rows], value_grad[rows:])
    vg_other = jnp.where(first, value_grad[rows:], value_grad[:rows])

    def outer(a, b):
        return lax.dot_general(a, b, (((0,), (0,)), ((), ())), preferred_element_type=jnp.float32)

    term = outer(hidden, vg_own) + outer(hidden_got, vg_other)

    term = term.astype(jnp.bfloat16).reshape(nx, nz * ny, -1, kv)
    term = jnp.sum(lax.all_to_all(term, "x", 0, 0).astype(jnp.float32), axis=0)
    term = term.astype(jnp.bfloat16).reshape(nz, ny, -1, kv).transpose(1, 0, 2, 3)
    term = jnp.sum(lax.all_to_all(term, "y", 0, 0).astype(jnp.float32), axis=0)
    keep = jnp.where(low, term[0], term[1])
    term = keep + lax.ppermute(jnp.where(low, term[1], term[0]), "zh", SWAP)
    cut = term.shape[0] // 2
    mine = jnp.where(first, term[:cut], term[cut:])
    theirs = lax.ppermute(jnp.where(first, term[cut:], term[:cut]), "c", SWAP)
    weight_grad = ordered(first, mine, theirs, axis=1)

    def project(a):
        return jnp.dot(a, w_full, preferred_element_type=jnp.float32).astype(jnp.bfloat16)

    v_chip = ordered(first, project(hidden), project(hidden_got))
    v_win = jnp.concatenate([chip_shift(v_chip, 2), chip_shift(v_chip, 1), v_chip], axis=0)
    v_two = jnp.stack([v_win[:span], v_win[rows : rows + span]])
    output = jnp.einsum("bgtl,bld->btgd", probs, v_two, preferred_element_type=jnp.float32)
    output = output.astype(jnp.bfloat16).reshape(2, rows, qw)
    out_own = jnp.where(first, output[0], output[1])
    out_got = lax.ppermute(jnp.where(first, output[1], output[0]), "c", SWAP)
    attention = ordered(first, out_own, out_got, axis=1)
    return attention, weight_grad


def solution(mesh):
    sizes = SIZES
    fine = Mesh(mesh.devices.reshape(*sizes, mesh.devices.shape[1]), (*GRID, "wt"))
    both = P(GRID, "wt")
    return jax.shard_map(
        per_device,
        mesh=fine,
        in_specs=(P(GRID, None), both, both, both, both, P()),
        out_specs=(both, both),
        check_vma=False,
    )
```

```python
import functools
import math

import jax
import jax.numpy as jnp
from jax import lax
from jax.experimental import pallas as pl
from jax.experimental.pallas import tpu as pltpu
from jax.sharding import Mesh, PartitionSpec as P

HD = 128
WINDOW = 1024
GRID = ("x", "zh", "y", "c")
CHIPS = ("x", "zh", "y")
SWAP = [(0, 1), (1, 0)]
SIZES = (4, 2, 8, 2)
BF16, F32 = jnp.bfloat16, jnp.float32
VMEM = pl.BlockSpec(memory_space=pltpu.VMEM)
SMEM = pl.BlockSpec(memory_space=pltpu.SMEM)


def struct(shape, dtype):
    return jax.ShapeDtypeStruct(shape, dtype)


def dot(a, b, over_a, over_b):
    return lax.dot_general(a, b, (((over_a,), (over_b,)), ((), ())), preferred_element_type=F32)


def chip_shift(block, distance):
    chips = lax.axis_size("x") * lax.axis_size("zh") * lax.axis_size("y")
    route = [(i - distance, i) for i in range(chips) if 0 <= i - distance < chips]
    return lax.ppermute(block, CHIPS, route)


def ordered(first, own, other, axis=0):
    return jnp.concatenate(
        [jnp.where(first, own, other), jnp.where(first, other, own)], axis=axis
    )


def attend_kernel(rows, factor, q_ref, k2_ref, k1_ref, k0_ref, g_ref, low_ref, *rest):
    probs_ref, part2_ref, part1_ref, part0_ref, win, total = rest
    chip_rows = 2 * rows
    span = win.shape[0] - rows
    group = q_ref.shape[1] // HD
    for i, ref in enumerate((k2_ref, k1_ref, k0_ref)):
        win[i * chip_rows : (i + 1) * chip_rows] = ref[...]
    total[span:] = jnp.zeros((rows, HD), F32)
    for j in range(2):
        at = slice(j * rows, j * rows + span)
        keys = win[at]
        u = lax.broadcasted_iota(jnp.int32, (span, rows), 0) + j * rows
        t = lax.broadcasted_iota(jnp.int32, (span, rows), 1) + (2 * chip_rows + j * rows)
        allowed = (u <= t) & (u >= low_ref[:, j * rows : (j + 1) * rows])
        for h in range(group):
            tile = (slice(j * rows, (j + 1) * rows), slice(h * HD, (h + 1) * HD))
            s = jnp.where(allowed, dot(keys, q_ref[tile], 1, 1), -1e30)
            w = jnp.exp2((s - jnp.max(s, axis=0, keepdims=True)) * factor)
            p = (w * (1.0 / jnp.sum(w, axis=0, keepdims=True))).astype(BF16)
            probs_ref[j, h] = p
            part = jnp.dot(p, g_ref[tile], preferred_element_type=F32)
            if j == 0 and h == 0:
                total[at] = part
            else:
                total[at] += part
    part2_ref[...] = total[:chip_rows].astype(BF16)
    part1_ref[...] = total[chip_rows : 2 * chip_rows].astype(BF16)
    part0_ref[...] = total[2 * chip_rows :]


def output_kernel(rows, core_ref, probs_ref, v2_ref, v1_ref, v0_ref, out_ref, win):
    chip_rows = 2 * rows
    span = win.shape[0] - rows
    for i, ref in enumerate((v2_ref, v1_ref, v0_ref)):
        win[i * chip_rows : (i + 1) * chip_rows] = ref[...]
    for j in range(2):
        slot = core_ref[0] if j == 0 else 1 - core_ref[0]
        values = win[j * rows : j * rows + span]
        for h in range(probs_ref.shape[1]):
            o = dot(values, probs_ref[j, h], 0, 0)
            out_ref[slot, :, h * HD : (h + 1) * HD] = o.T.astype(BF16)


def outer_kernel(rows, core_ref, own_ref, got_ref, part_ref, back1_ref, back2_ref, out_ref, vg):
    vg[...] = (part_ref[...] + back1_ref[...].astype(F32) + back2_ref[...].astype(F32)).astype(BF16)
    mine = pl.multiple_of(core_ref[0] * rows, rows)
    a = vg[pl.ds(mine, rows)]
    b = vg[pl.ds(pl.multiple_of(rows - mine, rows), rows)]
    width = 3 * HD
    for i in range(0, own_ref.shape[1], width):
        at = slice(i, min(i + width, own_ref.shape[1]))
        t = dot(a, own_ref[:, at], 0, 0) + dot(b, got_ref[:, at], 0, 0)
        out_ref[at] = t.T.astype(BF16)


def per_device(hidden, weight, queries, keys, grads, segments):
    rows = hidden.shape[0]
    chip_rows = 2 * rows
    kv = weight.shape[1] // 2
    qw = queries.shape[1] // 2
    group = qw // kv
    cut = weight.shape[0]
    nx, nz, ny = (lax.axis_size(a) for a in CHIPS)
    core = lax.axis_index("c")
    first = core == 0
    low = lax.axis_index("zh") == 0
    chip = (lax.axis_index("x") * nz + lax.axis_index("zh")) * ny + lax.axis_index("y")
    factor = math.log2(math.e) / math.sqrt(HD)
    span = WINDOW + rows
    whole = span + rows
    core_arg = core.astype(jnp.int32)[None]

    def halves(a):
        w = a.shape[1] // 2
        return jnp.where(first, a[:, :w], a[:, w:]), jnp.where(first, a[:, w:], a[:, :w])

    k_own, k_send = halves(keys)
    q_own, q_send = halves(queries)
    g_own, g_send = halves(grads)
    w_own, w_send = halves(weight)
    tall = ((0, rows - cut), (0, 0))

    send = jnp.concatenate([k_send, q_send, g_send, jnp.pad(w_send, tall)], axis=1)
    got = lax.ppermute(send, "c", SWAP)
    k_chip = ordered(first, k_own, got[:, :kv])
    k_two = chip_shift(k_chip, 2)
    k_one = chip_shift(k_chip, 1)
    q_chip = ordered(first, q_own, got[:, kv : kv + qw])
    g_chip = ordered(first, g_own, got[:, kv + qw : kv + 2 * qw])

    w_chip = ordered(first, w_own, got[:cut, kv + 2 * qw :])
    w_far = lax.ppermute(w_chip, "zh", SWAP)
    w_pair = ordered(low, w_chip[None], w_far[None])
    w_y = lax.all_to_all(jnp.broadcast_to(w_pair[None], (ny, *w_pair.shape)), "y", 0, 0)
    w_y = w_y.transpose(1, 0, 2, 3).reshape(-1, kv)
    w_x = lax.all_to_all(jnp.broadcast_to(w_y[None], (nx, *w_y.shape)), "x", 0, 0)
    w_full = w_x.reshape(-1, kv)

    hidden_got = lax.ppermute(hidden, "c", SWAP)

    padding = 2 * chip_rows
    padded = jnp.concatenate([jnp.full((padding,), -1, jnp.int32), segments], axis=0)
    seg_win = lax.dynamic_slice_in_dim(padded, chip * chip_rows, whole, 0)
    begin = jnp.sum((seg_win[:, None] < seg_win[None, padding:]).astype(jnp.int32), axis=0)
    begin = jnp.maximum(begin, jnp.arange(chip_rows, dtype=jnp.int32) + (padding - WINDOW + 1))

    probs, part2, part1, part0 = pl.pallas_call(
        functools.partial(attend_kernel, rows, factor),
        out_shape=(
            struct((2, group, span, rows), BF16),
            struct((chip_rows, kv), BF16),
            struct((chip_rows, kv), BF16),
            struct((chip_rows, kv), F32),
        ),
        in_specs=[VMEM] * 6,
        out_specs=[VMEM] * 4,
        scratch_shapes=[pltpu.VMEM((whole, kv), BF16), pltpu.VMEM((whole, kv), F32)],
    )(q_chip, k_two, k_one, k_chip, g_chip, begin[None])
    back2 = chip_shift(part2, -2)
    back1 = chip_shift(part1, -1)

    v_own = jnp.dot(hidden, w_full, preferred_element_type=F32).astype(BF16)
    v_other = jnp.dot(hidden_got, w_full, preferred_element_type=F32).astype(BF16)
    v_chip = ordered(first, v_own, v_other)
    v_two = chip_shift(v_chip, 2)
    v_one = chip_shift(v_chip, 1)

    term = pl.pallas_call(
        functools.partial(outer_kernel, rows),
        out_shape=struct((hidden.shape[1], kv), BF16),
        in_specs=[SMEM] + [VMEM] * 5,
        out_specs=VMEM,
        scratch_shapes=[pltpu.VMEM((chip_rows, kv), BF16)],
    )(core_arg, hidden, hidden_got, part0, back1, back2)

    term = lax.all_to_all(term.reshape(nx, -1, kv), "x", 0, 0)
    term = jnp.sum(term.astype(F32), axis=0).astype(BF16)
    term = term.reshape(nz, ny, 2 * cut, kv).transpose(1, 0, 2, 3)
    term = lax.all_to_all(term, "y", 0, 0)
    term = jnp.sum(term.astype(F32), axis=0)
    keep = jnp.where(low, term[0], term[1])
    far = lax.ppermute(jnp.where(low, term[1], term[0]), "zh", SWAP)
    term = keep + far
    mine = jnp.where(first, term[:cut], term[cut:])
    theirs = lax.ppermute(jnp.where(first, term[cut:], term[:cut]), "c", SWAP)
    weight_grad = ordered(first, mine, theirs, axis=1)

    output = pl.pallas_call(
        functools.partial(output_kernel, rows),
        out_shape=struct((2, rows, qw), BF16),
        in_specs=[SMEM] + [VMEM] * 4,
        out_specs=VMEM,
        scratch_shapes=[pltpu.VMEM((whole, kv), BF16)],
    )(core_arg, probs, v_two, v_one, v_chip)
    out_got = lax.ppermute(output[1], "c", SWAP)
    attention = ordered(first, output[0], out_got, axis=1)
    return attention, weight_grad


def solution(mesh):
    fine = Mesh(mesh.devices.reshape(*SIZES, mesh.devices.shape[1]), (*GRID, "wt"))
    both = P(GRID, "wt")
    return jax.shard_map(
        per_device,
        mesh=fine,
        in_specs=(P(GRID, None), both, both, both, both, P()),
        out_specs=(both, both),
        check_vma=False,
    )
```

```python
import functools
import math

import jax
import jax.numpy as jnp
from jax import lax
from jax.experimental import pallas as pl
from jax.experimental.pallas import tpu as pltpu
from jax.sharding import Mesh, PartitionSpec as P

HD = 128
WINDOW = 1024
GRID = ("x", "zh", "y", "c")
CHIPS = ("x", "zh", "y")
SWAP = [(0, 1), (1, 0)]
SIZES = (4, 2, 8, 2)
BF16, F32 = jnp.bfloat16, jnp.float32
VMEM = pl.BlockSpec(memory_space=pltpu.VMEM)
SMEM = pl.BlockSpec(memory_space=pltpu.SMEM)


def struct(shape, dtype):
    return jax.ShapeDtypeStruct(shape, dtype)


def dot(a, b, over_a, over_b):
    return lax.dot_general(a, b, (((over_a,), (over_b,)), ((), ())), preferred_element_type=F32)


def chip_shift(block, distance):
    chips = lax.axis_size("x") * lax.axis_size("zh") * lax.axis_size("y")
    route = [(i - distance, i) for i in range(chips) if 0 <= i - distance < chips]
    return lax.ppermute(block, CHIPS, route)


def ordered(first, own, other, axis=0):
    return jnp.concatenate(
        [jnp.where(first, own, other), jnp.where(first, other, own)], axis=axis
    )


def prepare_kernel(core_ref, k_ref, q_ref, g_ref, w_ref, out_ref):
    other = 1 - core_ref[0]
    at = 0
    for ref in (k_ref, q_ref, g_ref, w_ref):
        width = ref.shape[1] // 2
        out_ref[: ref.shape[0], at : at + width] = ref[:, part_of(other, width)]
        at += width
    out_ref[w_ref.shape[0] :, at - width :] = jnp.zeros(
        (out_ref.shape[0] - w_ref.shape[0], width), out_ref.dtype
    )


def part_of(index, size):
    return pl.ds(pl.multiple_of(index * size, size), size)


def attend_kernel(rows, factor, core_ref, *refs):
    k_ref, q_ref, g_ref, got_ref, k2_ref, k1_ref, low_ref = refs[:7]
    probs_ref, part2_ref, part1_ref, part0_ref, win, total = refs[7:]
    chip_rows = 2 * rows
    span = win.shape[0] - rows
    kv, qw = k_ref.shape[1] // 2, q_ref.shape[1] // 2
    core = core_ref[0]
    win[:chip_rows] = k2_ref[...]
    win[chip_rows : 2 * chip_rows] = k1_ref[...]
    home = win.at[2 * chip_rows :]
    home[part_of(core, rows)] = k_ref[:, part_of(core, kv)]
    home[part_of(1 - core, rows)] = got_ref[:, :kv]
    total[...] = jnp.zeros_like(total)
    u = lax.broadcasted_iota(jnp.int32, (span, rows), 0)
    t = lax.broadcasted_iota(jnp.int32, (span, rows), 1) + (span - rows)
    for slot in range(2):
        j = core if slot == 0 else 1 - core
        at = pl.ds(pl.multiple_of(j * rows, rows), span)
        keys = win[at]
        allowed = (u <= t) & (u >= low_ref[slot : slot + 1])
        for h in range(qw // HD):
            if slot == 0:
                q = q_ref[:, part_of(core * (qw // HD) + h, HD)]
                g = g_ref[:, part_of(core * (qw // HD) + h, HD)]
            else:
                q = got_ref[:, kv + h * HD : kv + (h + 1) * HD]
                g = got_ref[:, kv + qw + h * HD : kv + qw + (h + 1) * HD]
            s = jnp.where(allowed, dot(keys, q, 1, 1), -1e30)
            w = jnp.exp2((s - jnp.max(s, axis=0, keepdims=True)) * factor)
            p = (w * (1.0 / jnp.sum(w, axis=0, keepdims=True))).astype(BF16)
            probs_ref[slot, h] = p
            total[at] += dot(p, g, 1, 0)
    part2_ref[...] = total[:chip_rows].astype(BF16)
    part1_ref[...] = total[chip_rows : 2 * chip_rows].astype(BF16)
    part0_ref[...] = total[2 * chip_rows :]


def output_kernel(rows, core_ref, probs_ref, v2_ref, v1_ref, v0_ref, out_ref, win):
    chip_rows = 2 * rows
    span = win.shape[0] - rows
    for i, ref in enumerate((v2_ref, v1_ref, v0_ref)):
        win[i * chip_rows : (i + 1) * chip_rows] = ref[...]
    for slot in range(2):
        j = core_ref[0] if slot == 0 else 1 - core_ref[0]
        values = win[pl.ds(pl.multiple_of(j * rows, rows), span)]
        for h in range(probs_ref.shape[1]):
            o = dot(values, probs_ref[slot, h], 0, 0)
            out_ref[slot, :, h * HD : (h + 1) * HD] = o.T.astype(BF16)


def outer_kernel(rows, core_ref, own_ref, got_ref, part_ref, back1_ref, back2_ref, out_ref, vg):
    vg[...] = (part_ref[...] + back1_ref[...].astype(F32) + back2_ref[...].astype(F32)).astype(BF16)
    mine = pl.multiple_of(core_ref[0] * rows, rows)
    a = vg[pl.ds(mine, rows)]
    b = vg[pl.ds(pl.multiple_of(rows - mine, rows), rows)]
    width = 3 * HD
    for i in range(0, own_ref.shape[1], width):
        at = slice(i, min(i + width, own_ref.shape[1]))
        t = dot(a, own_ref[:, at], 0, 0) + dot(b, got_ref[:, at], 0, 0)
        out_ref[at] = t.T.astype(BF16)


def per_device(hidden, weight, queries, keys, grads, segments):
    rows = hidden.shape[0]
    chip_rows = 2 * rows
    kv = weight.shape[1] // 2
    qw = queries.shape[1] // 2
    group = qw // kv
    cut = weight.shape[0]
    nx, nz, ny = (lax.axis_size(a) for a in CHIPS)
    core = lax.axis_index("c")
    first = core == 0
    low = lax.axis_index("zh") == 0
    chip = (lax.axis_index("x") * nz + lax.axis_index("zh")) * ny + lax.axis_index("y")
    factor = math.log2(math.e) / math.sqrt(HD)
    span = WINDOW + rows
    whole = span + rows
    core_arg = core.astype(jnp.int32)[None]

    def mine_of(a):
        w = a.shape[1] // 2
        return jnp.where(first, a[:, :w], a[:, w:])

    send = pl.pallas_call(
        prepare_kernel,
        out_shape=struct((rows, 2 * kv + 2 * qw), BF16),
        in_specs=[SMEM] + [VMEM] * 4,
        out_specs=VMEM,
    )(core_arg, keys, queries, grads, weight)
    got = lax.ppermute(send, "c", SWAP)
    k_chip = ordered(first, mine_of(keys), got[:, :kv])
    k_two = chip_shift(k_chip, 2)
    k_one = chip_shift(k_chip, 1)

    w_chip = ordered(first, mine_of(weight), got[:cut, kv + 2 * qw :])
    w_far = lax.ppermute(w_chip, "zh", SWAP)
    w_pair = ordered(low, w_chip[None], w_far[None])
    w_y = lax.all_to_all(jnp.broadcast_to(w_pair[None], (ny, *w_pair.shape)), "y", 0, 0)
    w_y = w_y.transpose(1, 0, 2, 3).reshape(-1, kv)
    w_x = lax.all_to_all(jnp.broadcast_to(w_y[None], (nx, *w_y.shape)), "x", 0, 0)
    w_full = w_x.reshape(-1, kv)

    hidden_got = lax.ppermute(hidden, "c", SWAP)

    padding = 2 * chip_rows
    padded = jnp.concatenate([jnp.full((padding,), -1, jnp.int32), segments], axis=0)
    seg_win = lax.dynamic_slice_in_dim(padded, chip * chip_rows, whole, 0)
    begin = jnp.sum((seg_win[:, None] < seg_win[None, padding:]).astype(jnp.int32), axis=0)
    begin = begin.reshape(2, rows) - rows * jnp.arange(2, dtype=jnp.int32)[:, None]
    begin = jnp.maximum(begin, jnp.arange(1, rows + 1, dtype=jnp.int32)[None])
    begin = jnp.where(first, begin, begin[::-1])

    probs, part2, part1, part0 = pl.pallas_call(
        functools.partial(attend_kernel, rows, factor),
        out_shape=(
            struct((2, group, span, rows), BF16),
            struct((chip_rows, kv), BF16),
            struct((chip_rows, kv), BF16),
            struct((chip_rows, kv), F32),
        ),
        in_specs=[SMEM] + [VMEM] * 7,
        out_specs=[VMEM] * 4,
        scratch_shapes=[pltpu.VMEM((whole, kv), BF16), pltpu.VMEM((whole, kv), F32)],
    )(core_arg, keys, queries, grads, got, k_two, k_one, begin)
    back2 = chip_shift(part2, -2)
    back1 = chip_shift(part1, -1)

    v_own = jnp.dot(hidden, w_full, preferred_element_type=F32).astype(BF16)
    v_other = jnp.dot(hidden_got, w_full, preferred_element_type=F32).astype(BF16)
    v_chip = ordered(first, v_own, v_other)
    v_two = chip_shift(v_chip, 2)
    v_one = chip_shift(v_chip, 1)

    term = pl.pallas_call(
        functools.partial(outer_kernel, rows),
        out_shape=struct((hidden.shape[1], kv), BF16),
        in_specs=[SMEM] + [VMEM] * 5,
        out_specs=VMEM,
        scratch_shapes=[pltpu.VMEM((chip_rows, kv), BF16)],
    )(core_arg, hidden, hidden_got, part0, back1, back2)

    term = lax.all_to_all(term.reshape(nx, -1, kv), "x", 0, 0)
    term = jnp.sum(term.astype(F32), axis=0).astype(BF16)
    term = lax.all_to_all(term.reshape(nz * ny * 2, cut, kv), ("zh", "y", "c"), 0, 0)
    term = jnp.sum(term.astype(F32).reshape(nz * ny, 2, cut, kv), axis=0)
    weight_grad = jnp.concatenate([term[0], term[1]], axis=1)

    output = pl.pallas_call(
        functools.partial(output_kernel, rows),
        out_shape=struct((2, rows, qw), BF16),
        in_specs=[SMEM] + [VMEM] * 4,
        out_specs=VMEM,
        scratch_shapes=[pltpu.VMEM((whole, kv), BF16)],
    )(core_arg, probs, v_two, v_one, v_chip)
    out_got = lax.ppermute(output[1], "c", SWAP)
    attention = ordered(first, output[0], out_got, axis=1)
    return attention, weight_grad


def solution(mesh):
    fine = Mesh(mesh.devices.reshape(*SIZES, mesh.devices.shape[1]), (*GRID, "wt"))
    both = P(GRID, "wt")
    return jax.shard_map(
        per_device,
        mesh=fine,
        in_specs=(P(GRID, None), both, both, both, both, P()),
        out_specs=(both, both),
        check_vma=False,
    )
```

```python
import functools
import math

import jax
import jax.numpy as jnp
from jax import lax
from jax.experimental import pallas as pl
from jax.experimental.pallas import tpu as pltpu
from jax.sharding import Mesh, PartitionSpec as P

HD = 128
WINDOW = 1024
GRID = ("x", "zh", "y", "c")
CHIPS = ("x", "zh", "y")
SWAP = [(0, 1), (1, 0)]
SIZES = (4, 2, 8, 2)
BF16, F32 = jnp.bfloat16, jnp.float32
VMEM = pl.BlockSpec(memory_space=pltpu.VMEM)
SMEM = pl.BlockSpec(memory_space=pltpu.SMEM)


def struct(shape, dtype):
    return jax.ShapeDtypeStruct(shape, dtype)


def dot(a, b, over_a, over_b):
    return lax.dot_general(a, b, (((over_a,), (over_b,)), ((), ())), preferred_element_type=F32)


def chip_shift(block, distance):
    chips = lax.axis_size("x") * lax.axis_size("zh") * lax.axis_size("y")
    route = [(i - distance, i) for i in range(chips) if 0 <= i - distance < chips]
    return lax.ppermute(block, CHIPS, route)


def ordered(first, own, other, axis=0):
    return jnp.concatenate(
        [jnp.where(first, own, other), jnp.where(first, other, own)], axis=axis
    )


def prepare_kernel(core_ref, k_ref, q_ref, g_ref, out_ref):
    other = 1 - core_ref[0]
    at = 0
    for ref in (k_ref, q_ref, g_ref):
        width = ref.shape[1] // 2
        out_ref[:, at : at + width] = ref[:, part_of(other, width)]
        at += width


def part_of(index, size):
    return pl.ds(pl.multiple_of(index * size, size), size)


def attend_kernel(rows, factor, core_ref, *refs):
    k_ref, q_ref, g_ref, got_ref, k2_ref, k1_ref, low_ref = refs[:7]
    probs_ref, part2_ref, part1_ref, part0_ref, win, total = refs[7:]
    chip_rows = 2 * rows
    span = win.shape[0] - rows
    kv, qw = k_ref.shape[1] // 2, q_ref.shape[1] // 2
    core = core_ref[0]
    win[:chip_rows] = k2_ref[...]
    win[chip_rows : 2 * chip_rows] = k1_ref[...]
    home = win.at[2 * chip_rows :]
    home[part_of(core, rows)] = k_ref[:, part_of(core, kv)]
    home[part_of(1 - core, rows)] = got_ref[:, :kv]
    total[...] = jnp.zeros_like(total)
    u = lax.broadcasted_iota(jnp.int32, (span, rows), 0)
    t = lax.broadcasted_iota(jnp.int32, (span, rows), 1) + (span - rows)
    for slot in range(2):
        j = core if slot == 0 else 1 - core
        at = pl.ds(pl.multiple_of(j * rows, rows), span)
        keys = win[at]
        allowed = (u <= t) & (u >= low_ref[slot : slot + 1])
        for h in range(qw // HD):
            if slot == 0:
                q = q_ref[:, part_of(core * (qw // HD) + h, HD)]
                g = g_ref[:, part_of(core * (qw // HD) + h, HD)]
            else:
                q = got_ref[:, kv + h * HD : kv + (h + 1) * HD]
                g = got_ref[:, kv + qw + h * HD : kv + qw + (h + 1) * HD]
            s = jnp.where(allowed, dot(keys, q, 1, 1), -1e30)
            w = jnp.exp2((s - jnp.max(s, axis=0, keepdims=True)) * factor)
            p = (w * (1.0 / jnp.sum(w, axis=0, keepdims=True))).astype(BF16)
            probs_ref[slot, h] = p
            total[at] += dot(p, g, 1, 0)
    part2_ref[...] = total[:chip_rows].astype(BF16)
    part1_ref[...] = total[chip_rows : 2 * chip_rows].astype(BF16)
    part0_ref[...] = total[2 * chip_rows :]


def output_kernel(rows, core_ref, probs_ref, v2_ref, v1_ref, v0_ref, out_ref, win):
    chip_rows = 2 * rows
    span = win.shape[0] - rows
    for i, ref in enumerate((v2_ref, v1_ref, v0_ref)):
        win[i * chip_rows : (i + 1) * chip_rows] = ref[...]
    for slot in range(2):
        j = core_ref[0] if slot == 0 else 1 - core_ref[0]
        values = win[pl.ds(pl.multiple_of(j * rows, rows), span)]
        for h in range(probs_ref.shape[1]):
            o = dot(values, probs_ref[slot, h], 0, 0)
            out_ref[slot, :, h * HD : (h + 1) * HD] = o.T.astype(BF16)


def outer_kernel(rows, core_ref, own_ref, got_ref, part_ref, back1_ref, back2_ref, out_ref, vg):
    vg[...] = (part_ref[...] + back1_ref[...].astype(F32) + back2_ref[...].astype(F32)).astype(BF16)
    mine = pl.multiple_of(core_ref[0] * rows, rows)
    a = vg[pl.ds(mine, rows)]
    b = vg[pl.ds(pl.multiple_of(rows - mine, rows), rows)]
    width = 3 * HD
    for i in range(0, own_ref.shape[1], width):
        at = slice(i, min(i + width, own_ref.shape[1]))
        t = dot(a, own_ref[:, at], 0, 0) + dot(b, got_ref[:, at], 0, 0)
        out_ref[at] = t.T.astype(BF16)


def per_device(hidden, weight, queries, keys, grads, segments):
    rows = hidden.shape[0]
    chip_rows = 2 * rows
    kv = weight.shape[1] // 2
    qw = queries.shape[1] // 2
    group = qw // kv
    cut = weight.shape[0]
    nx, nz, ny = (lax.axis_size(a) for a in CHIPS)
    core = lax.axis_index("c")
    first = core == 0
    chip = (lax.axis_index("x") * nz + lax.axis_index("zh")) * ny + lax.axis_index("y")
    factor = math.log2(math.e) / math.sqrt(HD)
    span = WINDOW + rows
    whole = span + rows
    core_arg = core.astype(jnp.int32)[None]

    def mine_of(a):
        w = a.shape[1] // 2
        return jnp.where(first, a[:, :w], a[:, w:])

    send = pl.pallas_call(
        prepare_kernel,
        out_shape=struct((rows, kv + 2 * qw), BF16),
        in_specs=[SMEM] + [VMEM] * 3,
        out_specs=VMEM,
    )(core_arg, keys, queries, grads)
    got = lax.ppermute(send, "c", SWAP)
    k_chip = ordered(first, mine_of(keys), got[:, :kv])
    k_two = chip_shift(k_chip, 2)
    k_one = chip_shift(k_chip, 1)

    tile = weight.reshape(cut, 2, kv).transpose(1, 0, 2)[None]
    tile = jnp.broadcast_to(tile, (nz * ny, *tile.shape[1:])).reshape(-1, cut, kv)
    w_y = lax.all_to_all(tile, ("zh", "y", "c"), 0, 0).reshape(-1, kv)
    w_x = lax.all_to_all(jnp.broadcast_to(w_y[None], (nx, *w_y.shape)), "x", 0, 0)
    w_full = w_x.reshape(-1, kv)

    hidden_got = lax.ppermute(hidden, "c", SWAP)

    padding = 2 * chip_rows
    padded = jnp.concatenate([jnp.full((padding,), -1, jnp.int32), segments], axis=0)
    seg_win = lax.dynamic_slice_in_dim(padded, chip * chip_rows, whole, 0)
    begin = jnp.sum((seg_win[:, None] < seg_win[None, padding:]).astype(jnp.int32), axis=0)
    begin = begin.reshape(2, rows) - rows * jnp.arange(2, dtype=jnp.int32)[:, None]
    begin = jnp.maximum(begin, jnp.arange(1, rows + 1, dtype=jnp.int32)[None])
    begin = jnp.where(first, begin, begin[::-1])

    probs, part2, part1, part0 = pl.pallas_call(
        functools.partial(attend_kernel, rows, factor),
        out_shape=(
            struct((2, group, span, rows), BF16),
            struct((chip_rows, kv), BF16),
            struct((chip_rows, kv), BF16),
            struct((chip_rows, kv), F32),
        ),
        in_specs=[SMEM] + [VMEM] * 7,
        out_specs=[VMEM] * 4,
        scratch_shapes=[pltpu.VMEM((whole, kv), BF16), pltpu.VMEM((whole, kv), F32)],
    )(core_arg, keys, queries, grads, got, k_two, k_one, begin)
    back2 = chip_shift(part2, -2)
    back1 = chip_shift(part1, -1)

    v_own = jnp.dot(hidden, w_full, preferred_element_type=F32).astype(BF16)
    v_other = jnp.dot(hidden_got, w_full, preferred_element_type=F32).astype(BF16)
    v_chip = ordered(first, v_own, v_other)
    v_two = chip_shift(v_chip, 2)
    v_one = chip_shift(v_chip, 1)

    term = pl.pallas_call(
        functools.partial(outer_kernel, rows),
        out_shape=struct((hidden.shape[1], kv), BF16),
        in_specs=[SMEM] + [VMEM] * 5,
        out_specs=VMEM,
        scratch_shapes=[pltpu.VMEM((chip_rows, kv), BF16)],
    )(core_arg, hidden, hidden_got, part0, back1, back2)

    term = lax.all_to_all(term.reshape(nx, -1, kv), "x", 0, 0)
    term = jnp.sum(term.astype(F32), axis=0).astype(BF16)
    term = lax.all_to_all(term.reshape(nz * ny * 2, cut, kv), ("zh", "y", "c"), 0, 0)
    term = jnp.sum(term.astype(F32).reshape(nz * ny, 2, cut, kv), axis=0)
    weight_grad = jnp.concatenate([term[0], term[1]], axis=1)

    output = pl.pallas_call(
        functools.partial(output_kernel, rows),
        out_shape=struct((2, rows, qw), BF16),
        in_specs=[SMEM] + [VMEM] * 4,
        out_specs=VMEM,
        scratch_shapes=[pltpu.VMEM((whole, kv), BF16)],
    )(core_arg, probs, v_two, v_one, v_chip)
    out_got = lax.ppermute(output[1], "c", SWAP)
    attention = ordered(first, output[0], out_got, axis=1)
    return attention, weight_grad


def solution(mesh):
    fine = Mesh(mesh.devices.reshape(*SIZES, mesh.devices.shape[1]), (*GRID, "wt"))
    both = P(GRID, "wt")
    return jax.shard_map(
        per_device,
        mesh=fine,
        in_specs=(P(GRID, None), both, both, both, both, P()),
        out_specs=(both, both),
        check_vma=False,
    )
```

```python
import functools
import math

import jax
import jax.numpy as jnp
from jax import lax
from jax.experimental import pallas as pl
from jax.experimental.pallas import tpu as pltpu
from jax.sharding import Mesh, PartitionSpec as P

HD = 128
WINDOW = 1024
GRID = ("x", "zh", "y", "c")
CHIPS = ("x", "zh", "y")
SWAP = [(0, 1), (1, 0)]
SIZES = (4, 2, 8, 2)
BF16, F32 = jnp.bfloat16, jnp.float32
VMEM = pl.BlockSpec(memory_space=pltpu.VMEM)
SMEM = pl.BlockSpec(memory_space=pltpu.SMEM)


def struct(shape, dtype):
    return jax.ShapeDtypeStruct(shape, dtype)


def dot(a, b, over_a, over_b):
    return lax.dot_general(a, b, (((over_a,), (over_b,)), ((), ())), preferred_element_type=F32)


def chip_shift(block, distance):
    chips = lax.axis_size("x") * lax.axis_size("zh") * lax.axis_size("y")
    route = [(i - distance, i) for i in range(chips) if 0 <= i - distance < chips]
    return lax.ppermute(block, CHIPS, route)


def ordered(core, own, other):
    slot = lax.broadcasted_iota(jnp.int32, (2, *own.shape), 0)
    both = jnp.where(slot == core, own[None], other[None])
    return both.reshape(-1, *own.shape[1:])


def prepare_kernel(core_ref, q_ref, g_ref, out_ref):
    other = 1 - core_ref[0]
    at = 0
    for ref in (q_ref, g_ref):
        width = ref.shape[1] // 2
        out_ref[:, at : at + width] = ref[:, part_of(other, width)]
        at += width


def part_of(index, size):
    return pl.ds(pl.multiple_of(index * size, size), size)


def attend_kernel(rows, factor, core_ref, *refs):
    k2_ref, k1_ref, k0_ref, q_ref, g_ref, got_ref, low_ref = refs[:7]
    probs_ref, part2_ref, part1_ref, part0_ref, win, total = refs[7:]
    chip_rows = 2 * rows
    span = win.shape[0] - rows
    qw = q_ref.shape[1] // 2
    core = core_ref[0]
    for i, ref in enumerate((k2_ref, k1_ref, k0_ref)):
        win[i * chip_rows : (i + 1) * chip_rows] = ref[...]
    total[...] = jnp.zeros_like(total)
    u = lax.broadcasted_iota(jnp.int32, (span, rows), 0)
    t = lax.broadcasted_iota(jnp.int32, (span, rows), 1) + (span - rows)
    for slot in range(2):
        j = core if slot == 0 else 1 - core
        at = pl.ds(pl.multiple_of(j * rows, rows), span)
        keys = win[at]
        allowed = (u <= t) & (u >= low_ref[slot : slot + 1])
        for h in range(qw // HD):
            if slot == 0:
                q = q_ref[:, part_of(core * (qw // HD) + h, HD)]
                g = g_ref[:, part_of(core * (qw // HD) + h, HD)]
            else:
                q = got_ref[:, h * HD : (h + 1) * HD]
                g = got_ref[:, qw + h * HD : qw + (h + 1) * HD]
            s = jnp.where(allowed, dot(keys, q, 1, 1), -1e30)
            w = jnp.exp2((s - jnp.max(s, axis=0, keepdims=True)) * factor)
            p = (w * (1.0 / jnp.sum(w, axis=0, keepdims=True))).astype(BF16)
            probs_ref[slot, h] = p
            total[at] += dot(p, g, 1, 0)
    part2_ref[...] = total[:chip_rows].astype(BF16)
    part1_ref[...] = total[chip_rows : 2 * chip_rows].astype(BF16)
    part0_ref[...] = total[2 * chip_rows :]


def output_kernel(rows, slot, core_ref, probs_ref, v2_ref, v1_ref, v0_ref, *rest):
    *got, out_ref, win = rest
    chip_rows = 2 * rows
    span = win.shape[0] - rows
    width = probs_ref.shape[1] * HD
    core = core_ref[0]
    for i, ref in enumerate((v2_ref, v1_ref, v0_ref)):
        win[i * chip_rows : (i + 1) * chip_rows] = ref[...]
    j = core if slot == 0 else 1 - core
    values = win[pl.ds(pl.multiple_of(j * rows, rows), span)]
    out = [dot(values, probs_ref[slot, h], 0, 0).T for h in range(probs_ref.shape[1])]
    out = jnp.concatenate(out, axis=1).astype(BF16)
    if slot == 0:
        out_ref[:, part_of(core, width)] = out
        out_ref[:, part_of(1 - core, width)] = got[0][...]
    else:
        out_ref[...] = out


def outer_kernel(rows, core_ref, own_ref, got_ref, part_ref, back1_ref, back2_ref, out_ref, vg):
    vg[...] = (part_ref[...] + back1_ref[...].astype(F32) + back2_ref[...].astype(F32)).astype(BF16)
    mine = pl.multiple_of(core_ref[0] * rows, rows)
    a = vg[pl.ds(mine, rows)]
    b = vg[pl.ds(pl.multiple_of(rows - mine, rows), rows)]
    width = 3 * HD
    for i in range(0, own_ref.shape[1], width):
        at = slice(i, min(i + width, own_ref.shape[1]))
        t = dot(a, own_ref[:, at], 0, 0) + dot(b, got_ref[:, at], 0, 0)
        out_ref[at] = t.T.astype(BF16)


def per_device(hidden, weight, queries, keys, grads, segments):
    rows = hidden.shape[0]
    chip_rows = 2 * rows
    kv = weight.shape[1] // 2
    qw = queries.shape[1] // 2
    group = qw // kv
    cut = weight.shape[0]
    nx, nz, ny = (lax.axis_size(a) for a in CHIPS)
    core = lax.axis_index("c")
    first = core == 0
    chip = (lax.axis_index("x") * nz + lax.axis_index("zh")) * ny + lax.axis_index("y")
    factor = math.log2(math.e) / math.sqrt(HD)
    span = WINDOW + rows
    whole = span + rows
    core_arg = core.astype(jnp.int32)[None]

    k_got = lax.ppermute(jnp.where(first, keys[:, kv:], keys[:, :kv]), "c", SWAP)
    k_chip = ordered(core, jnp.where(first, keys[:, :kv], keys[:, kv:]), k_got)
    k_two = chip_shift(k_chip, 2)
    k_one = chip_shift(k_chip, 1)

    send = pl.pallas_call(
        prepare_kernel,
        out_shape=struct((rows, 2 * qw), BF16),
        in_specs=[SMEM] + [VMEM] * 2,
        out_specs=VMEM,
    )(core_arg, queries, grads)
    got = lax.ppermute(send, "c", SWAP)
    hidden_got = lax.ppermute(hidden, "c", SWAP)

    tile = weight.reshape(cut, 2, kv).transpose(1, 0, 2)[None]
    tile = jnp.broadcast_to(tile, (nz * ny, *tile.shape[1:])).reshape(-1, cut, kv)
    w_y = lax.all_to_all(tile, ("zh", "y", "c"), 0, 0).reshape(-1, kv)
    w_x = lax.all_to_all(jnp.broadcast_to(w_y[None], (nx, *w_y.shape)), "x", 0, 0)
    w_full = w_x.reshape(-1, kv)

    padding = 2 * chip_rows
    padded = jnp.concatenate([jnp.full((padding,), -1, jnp.int32), segments], axis=0)
    seg_win = lax.dynamic_slice_in_dim(padded, chip * chip_rows, whole, 0)
    begin = jnp.sum((seg_win[:, None] < seg_win[None, padding:]).astype(jnp.int32), axis=0)
    begin = begin.reshape(2, rows) - rows * jnp.arange(2, dtype=jnp.int32)[:, None]
    begin = jnp.maximum(begin, jnp.arange(1, rows + 1, dtype=jnp.int32)[None])
    begin = jnp.where(first, begin, begin[::-1])

    probs, part2, part1, part0 = pl.pallas_call(
        functools.partial(attend_kernel, rows, factor),
        out_shape=(
            struct((2, group, span, rows), BF16),
            struct((chip_rows, kv), BF16),
            struct((chip_rows, kv), BF16),
            struct((chip_rows, kv), F32),
        ),
        in_specs=[SMEM] + [VMEM] * 7,
        out_specs=[VMEM] * 4,
        scratch_shapes=[pltpu.VMEM((whole, kv), BF16), pltpu.VMEM((whole, kv), F32)],
    )(core_arg, k_two, k_one, k_chip, queries, grads, got, begin)
    back2 = chip_shift(part2, -2)
    back1 = chip_shift(part1, -1)

    v_own = jnp.dot(hidden, w_full, preferred_element_type=F32).astype(BF16)
    v_other = jnp.dot(hidden_got, w_full, preferred_element_type=F32).astype(BF16)
    v_chip = jnp.concatenate(
        [jnp.where(first, v_own, v_other), jnp.where(first, v_other, v_own)], axis=0
    )
    v_two = chip_shift(v_chip, 2)
    v_one = chip_shift(v_chip, 1)

    term = pl.pallas_call(
        functools.partial(outer_kernel, rows),
        out_shape=struct((hidden.shape[1], kv), BF16),
        in_specs=[SMEM] + [VMEM] * 5,
        out_specs=VMEM,
        scratch_shapes=[pltpu.VMEM((chip_rows, kv), BF16)],
    )(core_arg, hidden, hidden_got, part0, back1, back2)

    term = lax.all_to_all(term.reshape(nx, -1, kv), "x", 0, 0)
    term = jnp.sum(term.astype(F32), axis=0).astype(BF16)
    term = lax.all_to_all(term.reshape(nz * ny * 2, cut, kv), ("zh", "y", "c"), 0, 0)
    term = jnp.sum(term.astype(F32).reshape(nz * ny, 2, cut, kv), axis=0)
    weight_grad = jnp.concatenate([term[0], term[1]], axis=1)

    def outputs(slot, *got):
        return pl.pallas_call(
            functools.partial(output_kernel, rows, slot),
            out_shape=struct((rows, qw * (1 + len(got))), BF16),
            in_specs=[SMEM] + [VMEM] * (4 + len(got)),
            out_specs=VMEM,
            scratch_shapes=[pltpu.VMEM((whole, kv), BF16)],
        )(core_arg, probs, v_two, v_one, v_chip, *got)

    out_send = outputs(1)
    out_got = lax.ppermute(out_send, "c", SWAP)
    attention = outputs(0, out_got)
    return attention, weight_grad


def solution(mesh):
    fine = Mesh(mesh.devices.reshape(*SIZES, mesh.devices.shape[1]), (*GRID, "wt"))
    both = P(GRID, "wt")
    return jax.shard_map(
        per_device,
        mesh=fine,
        in_specs=(P(GRID, None), both, both, both, both, P()),
        out_specs=(both, both),
        check_vma=False,
    )
```

```python
import functools
import math

import jax
import jax.numpy as jnp
from jax import lax
from jax.experimental import pallas as pl
from jax.experimental.pallas import tpu as pltpu
from jax.sharding import Mesh, PartitionSpec as P

HD = 128
WINDOW = 1024
GRID = ("x", "zh", "y", "c")
CHIPS = ("x", "zh", "y")
SWAP = [(0, 1), (1, 0)]
SIZES = (4, 2, 8, 2)
BF16, F32 = jnp.bfloat16, jnp.float32
VMEM = pl.BlockSpec(memory_space=pltpu.VMEM)
SMEM = pl.BlockSpec(memory_space=pltpu.SMEM)


def struct(shape, dtype):
    return jax.ShapeDtypeStruct(shape, dtype)


def dot(a, b, over_a, over_b):
    return lax.dot_general(a, b, (((over_a,), (over_b,)), ((), ())), preferred_element_type=F32)


def chip_shift(block, distance):
    chips = lax.axis_size("x") * lax.axis_size("zh") * lax.axis_size("y")
    route = [(i - distance, i) for i in range(chips) if 0 <= i - distance < chips]
    return lax.ppermute(block, CHIPS, route)


def ordered(core, own, other):
    slot = lax.broadcasted_iota(jnp.int32, (2, *own.shape), 0)
    both = jnp.where(slot == core, own[None], other[None])
    return both.reshape(-1, *own.shape[1:])


def prepare_kernel(core_ref, q_ref, g_ref, out_ref):
    other = 1 - core_ref[0]
    at = 0
    for ref in (q_ref, g_ref):
        width = ref.shape[1] // 2
        out_ref[:, at : at + width] = ref[:, part_of(other, width)]
        at += width


def part_of(index, size):
    return pl.ds(pl.multiple_of(index * size, size), size)


def attend_kernel(rows, factor, core_ref, *refs):
    k2_ref, k1_ref, k0_ref, q_ref, g_ref, got_ref, low_ref = refs[:7]
    *probs_refs, part2_ref, part1_ref, part0_ref, win, total = refs[7:]
    chip_rows = 2 * rows
    span = win.shape[0] - rows
    qw = q_ref.shape[1] // 2
    core = core_ref[0]
    for i, ref in enumerate((k2_ref, k1_ref, k0_ref)):
        win[i * chip_rows : (i + 1) * chip_rows] = ref[...]
    total[...] = jnp.zeros_like(total)
    u = lax.broadcasted_iota(jnp.int32, (span, rows), 0)
    t = lax.broadcasted_iota(jnp.int32, (span, rows), 1) + (span - rows)
    for slot in range(2):
        j = core if slot == 0 else 1 - core
        at = pl.ds(pl.multiple_of(j * rows, rows), span)
        keys = win[at]
        allowed = (u <= t) & (u >= low_ref[slot : slot + 1])
        for h in range(qw // HD):
            if slot == 0:
                q = q_ref[:, part_of(core * (qw // HD) + h, HD)]
                g = g_ref[:, part_of(core * (qw // HD) + h, HD)]
            else:
                q = got_ref[:, h * HD : (h + 1) * HD]
                g = got_ref[:, qw + h * HD : qw + (h + 1) * HD]
            s = jnp.where(allowed, dot(keys, q, 1, 1), -1e30)
            w = jnp.exp2((s - jnp.max(s, axis=0, keepdims=True)) * factor)
            p = (w * (1.0 / jnp.sum(w, axis=0, keepdims=True))).astype(BF16)
            probs_refs[slot][h] = p
            total[at] += dot(p, g, 1, 0)
    part2_ref[...] = total[:chip_rows].astype(BF16)
    part1_ref[...] = total[chip_rows : 2 * chip_rows].astype(BF16)
    part0_ref[...] = total[2 * chip_rows :]


def output_kernel(rows, slot, core_ref, probs_ref, v2_ref, v1_ref, v0_ref, *rest):
    *got, out_ref, win = rest
    chip_rows = 2 * rows
    span = win.shape[0] - rows
    width = probs_ref.shape[0] * HD
    core = core_ref[0]
    for i, ref in enumerate((v2_ref, v1_ref, v0_ref)):
        win[i * chip_rows : (i + 1) * chip_rows] = ref[...]
    j = core if slot == 0 else 1 - core
    values = win[pl.ds(pl.multiple_of(j * rows, rows), span)]
    out = [dot(values, probs_ref[h], 0, 0).T for h in range(probs_ref.shape[0])]
    out = jnp.concatenate(out, axis=1).astype(BF16)
    if slot == 0:
        out_ref[:, part_of(core, width)] = out
        out_ref[:, part_of(1 - core, width)] = got[0][...]
    else:
        out_ref[...] = out


def outer_kernel(rows, core_ref, own_ref, got_ref, part_ref, back1_ref, back2_ref, out_ref, vg):
    vg[...] = (part_ref[...] + back1_ref[...].astype(F32) + back2_ref[...].astype(F32)).astype(BF16)
    mine = pl.multiple_of(core_ref[0] * rows, rows)
    a = vg[pl.ds(mine, rows)]
    b = vg[pl.ds(pl.multiple_of(rows - mine, rows), rows)]
    width = 3 * HD
    for i in range(0, own_ref.shape[1], width):
        at = slice(i, min(i + width, own_ref.shape[1]))
        t = dot(a, own_ref[:, at], 0, 0) + dot(b, got_ref[:, at], 0, 0)
        out_ref[at] = t.T.astype(BF16)


def per_device(hidden, weight, queries, keys, grads, segments):
    rows = hidden.shape[0]
    chip_rows = 2 * rows
    kv = weight.shape[1] // 2
    qw = queries.shape[1] // 2
    group = qw // kv
    cut = weight.shape[0]
    nx, nz, ny = (lax.axis_size(a) for a in CHIPS)
    core = lax.axis_index("c")
    first = core == 0
    chip = (lax.axis_index("x") * nz + lax.axis_index("zh")) * ny + lax.axis_index("y")
    factor = math.log2(math.e) / math.sqrt(HD)
    span = WINDOW + rows
    whole = span + rows
    core_arg = core.astype(jnp.int32)[None]

    k_got = lax.ppermute(jnp.where(first, keys[:, kv:], keys[:, :kv]), "c", SWAP)
    k_chip = ordered(core, jnp.where(first, keys[:, :kv], keys[:, kv:]), k_got)
    k_two = chip_shift(k_chip, 2)
    k_one = chip_shift(k_chip, 1)

    send = pl.pallas_call(
        prepare_kernel,
        out_shape=struct((rows, 2 * qw), BF16),
        in_specs=[SMEM] + [VMEM] * 2,
        out_specs=VMEM,
    )(core_arg, queries, grads)
    got = lax.ppermute(send, "c", SWAP)
    hidden_got = lax.ppermute(hidden, "c", SWAP)

    tile = weight.reshape(cut, 2, kv).transpose(1, 0, 2)[None]
    tile = jnp.broadcast_to(tile, (nz * ny, *tile.shape[1:])).reshape(-1, cut, kv)
    w_y = lax.all_to_all(tile, ("zh", "y", "c"), 0, 0).reshape(-1, kv)
    w_x = lax.all_to_all(jnp.broadcast_to(w_y[None], (nx, *w_y.shape)), "x", 0, 0)
    w_full = w_x.reshape(-1, kv)

    padding = 2 * chip_rows
    padded = jnp.concatenate([jnp.full((padding,), -1, jnp.int32), segments], axis=0)
    seg_win = lax.dynamic_slice_in_dim(padded, chip * chip_rows, whole, 0)
    begin = jnp.sum((seg_win[:, None] < seg_win[None, padding:]).astype(jnp.int32), axis=0)
    begin = begin.reshape(2, rows) - rows * jnp.arange(2, dtype=jnp.int32)[:, None]
    begin = jnp.maximum(begin, jnp.arange(1, rows + 1, dtype=jnp.int32)[None])
    begin = jnp.where(first, begin, begin[::-1])

    *probs, part2, part1, part0 = pl.pallas_call(
        functools.partial(attend_kernel, rows, factor),
        out_shape=(
            struct((group, span, rows), BF16),
            struct((group, span, rows), BF16),
            struct((chip_rows, kv), BF16),
            struct((chip_rows, kv), BF16),
            struct((chip_rows, kv), F32),
        ),
        in_specs=[SMEM] + [VMEM] * 7,
        out_specs=[VMEM] * 5,
        scratch_shapes=[pltpu.VMEM((whole, kv), BF16), pltpu.VMEM((whole, kv), F32)],
    )(core_arg, k_two, k_one, k_chip, queries, grads, got, begin)
    back2 = chip_shift(part2, -2)
    back1 = chip_shift(part1, -1)

    v_own = jnp.dot(hidden, w_full, preferred_element_type=F32).astype(BF16)
    v_other = jnp.dot(hidden_got, w_full, preferred_element_type=F32).astype(BF16)
    v_chip = jnp.concatenate(
        [jnp.where(first, v_own, v_other), jnp.where(first, v_other, v_own)], axis=0
    )
    v_two = chip_shift(v_chip, 2)
    v_one = chip_shift(v_chip, 1)

    term = pl.pallas_call(
        functools.partial(outer_kernel, rows),
        out_shape=struct((hidden.shape[1], kv), BF16),
        in_specs=[SMEM] + [VMEM] * 5,
        out_specs=VMEM,
        scratch_shapes=[pltpu.VMEM((chip_rows, kv), BF16)],
    )(core_arg, hidden, hidden_got, part0, back1, back2)

    term = lax.all_to_all(term.reshape(nx, -1, kv), "x", 0, 0)
    term = jnp.sum(term.astype(F32), axis=0).astype(BF16)
    term = term.reshape(nz, ny * 2, cut, kv).transpose(1, 0, 2, 3)
    term = lax.all_to_all(term, ("y", "c"), 0, 0)
    term = jnp.sum(term.astype(F32).reshape(ny, 2, nz, cut, kv), axis=0)
    term = jnp.concatenate([term[0], term[1]], axis=2)
    low = lax.axis_index("zh") == 0
    far = lax.ppermute(jnp.where(low, term[1], term[0]), "zh", SWAP)
    weight_grad = jnp.where(low, term[0], term[1]) + far

    def outputs(slot, *got):
        return pl.pallas_call(
            functools.partial(output_kernel, rows, slot),
            out_shape=struct((rows, qw * (1 + len(got))), BF16),
            in_specs=[SMEM] + [VMEM] * (4 + len(got)),
            out_specs=VMEM,
            scratch_shapes=[pltpu.VMEM((whole, kv), BF16)],
        )(core_arg, probs[slot], v_two, v_one, v_chip, *got)

    out_send = outputs(1)
    out_got = lax.ppermute(out_send, "c", SWAP)
    attention = outputs(0, out_got)
    return attention, weight_grad


def solution(mesh):
    fine = Mesh(mesh.devices.reshape(*SIZES, mesh.devices.shape[1]), (*GRID, "wt"))
    both = P(GRID, "wt")
    return jax.shard_map(
        per_device,
        mesh=fine,
        in_specs=(P(GRID, None), both, both, both, both, P()),
        out_specs=(both, both),
        check_vma=False,
    )
```
